32 devices in a mesh: mode: 8 (over y, x, core), rows: 4 (over z).
Axes of the slice: x: 2, y: 2, z: 4, core: 2. Of those that a mesh axis runs over, the one named last changes fastest.
Arguments:
- tangents: float32 [128, 3, 32, 1024], P('mode', None, 'rows'), may hold values from -6 to 6
- checkpoints: float32 [8, 3, 32, 1024], P(None, None, 'rows', 'mode'), may hold values from 0 to 0.5
- owner_order: int32 [8], replicated, may hold values from 0 to 7, each once
- land_mask: int32 [32, 1024], P('rows'), may hold values 0 or 1
- coefficients: float32 [128, 128], replicated, may hold values from -0.9 to 0.9
Outputs:
- vectors: float32 [128, 3, 32, 1024], P(None, None, 'rows', 'mode')
The draws below stay inside these ranges and needn't reach their ends.
Inputs may be any that keep to these rules, and one draw needn't show every extreme that they name: `owner_order`: every checkpoint slot is named by exactly one step.
All inputs are finite; a program needn't handle non-finite values. No bound on the sum of `land_mask` on one device may be relied on, other than what follows from the above.
Results may differ from the reference program's by a relative error of at most 0.0002.
Values sent between devices are 32-bit elements; how exact they have to be, the bound alone decides.
A program may use at most 64 MiB of HBM per device.

```python
import jax
import jax.numpy as jnp
from jax import lax

MODES = 128
NX = 1024
STEPS = 8
NY = 32


def touch_ends(entries, rng, low, largest):
    longest = entries.shape.index(max(entries.shape))
    spots = []
    for shift in (0, 1):
        where = [jax.random.randint(jax.random.fold_in(rng, axis), (), 0, length) for axis, length in enumerate(entries.shape)]
        where[longest] = (where[longest] + shift) % entries.shape[longest]
        spots.append(tuple(where))
    return entries.at[spots[0]].set(low).at[spots[1]].set(largest)


def levels(rng, extent, cuts, smallest, top_value):
    loudness = 1.0
    for dim, parts in cuts:
        steps = jax.random.uniform(jax.random.fold_in(jax.random.fold_in(rng, 6), dim), (parts,), jnp.float32, smallest / len(cuts), top_value / len(cuts))
        loudness = loudness * jnp.repeat(jnp.exp(steps), extent[dim] // parts).reshape((-1,) + (1,) * (len(extent) - 1 - dim))
    return loudness


def noise(stream_key, shape, spread, limit, split=(), kind=jnp.bfloat16):
    entries = spread * jax.random.normal(stream_key, shape, jnp.float32)
    if split:
        entries = entries * levels(stream_key, shape, split, -0.22, 0.18)
    return jnp.clip(entries, -limit, limit).astype(kind)


def setup_inputs(seed: int = 0) -> dict:
    streams_of = jax.random.split(jax.random.key(seed), 6)
    return {
        "tangents": noise(streams_of[0], (MODES, 3, NY, NX), 1.0, 6.0, ((0, 8), (2, 4)), jnp.float32),
        "checkpoints": jnp.clip(0.5 * jax.random.uniform(streams_of[1], (STEPS, 3, NY, NX), jnp.float32) ** levels(streams_of[1], (STEPS, 3, NY, NX), ((2, 4), (3, 8)), -0.2, 0.2), 0.0, 0.5),
        "owner_order": jax.random.permutation(streams_of[2], STEPS).astype(jnp.int32),
        "land_mask": touch_ends((jax.random.randint(streams_of[3], (NY, NX), 0, 5) < 4).astype(jnp.int32), jax.random.fold_in(streams_of[3], 1), 0, 1),
        "coefficients": noise(streams_of[4], (MODES, MODES), 0.15, 0.9, (), jnp.float32),
    }


mean_depth = 1.0
gravity = 1.0
coriolis = 0.5
time_step = 0.5


def deriv_x(values):
    return 0.5 * (jnp.roll(values, -1, -1) - jnp.roll(values, 1, -1))


def deriv_y(values):
    return 0.5 * (values[..., 2:, :] - values[..., :-2, :])


def interior(values):
    return values[..., 1:-1, :]


def tendency(base_flow, current):
    depth_total = mean_depth + base_flow[0]
    flow_u = base_flow[1]
    flow_v = base_flow[2]
    height = current[0]
    zonal = current[1]
    meridional = current[2]
    flux_x = depth_total * zonal + height * flow_u
    flux_y = depth_total * meridional + height * flow_v
    height_rate = -(interior(deriv_x(flux_x)) + deriv_y(flux_y))
    zonal_mid = interior(zonal)
    merid_mid = interior(meridional)
    flow_umid = interior(flow_u)
    flow_vmid = interior(flow_v)
    zonal_rate = -(flow_umid * interior(deriv_x(zonal)) + zonal_mid * interior(deriv_x(flow_u))
                   + flow_vmid * deriv_y(zonal) + merid_mid * deriv_y(flow_u)) + coriolis * merid_mid - gravity * interior(deriv_x(height))
    merid_rate = -(flow_umid * interior(deriv_x(meridional)) + zonal_mid * interior(deriv_x(flow_v))
                   + flow_vmid * deriv_y(meridional) + merid_mid * deriv_y(flow_v)) - coriolis * zonal_mid - gravity * deriv_y(height)
    return jnp.stack([height_rate, zonal_rate, merid_rate], 0)


def pad_rows(values):
    return jnp.pad(values, ((0, 0), (1, 1), (0, 0)))


def reference(tangents, checkpoints, owner_order, land_mask, coefficients):
    wet_mask = land_mask.astype(jnp.float32)

    def one_mode(initial):
        def advance(step_index, current):
            base_flow = lax.dynamic_index_in_dim(checkpoints, owner_order[step_index].astype(jnp.int32), 0, keepdims=False)
            padded_base = pad_rows(base_flow)
            slope_one = tendency(padded_base, pad_rows(current))
            middle = wet_mask * (current + time_step * slope_one)
            slope_two = tendency(padded_base, pad_rows(middle))
            return wet_mask * (current + 0.5 * time_step * (slope_one + slope_two))

        return lax.fori_loop(0, STEPS, advance, wet_mask * initial)

    final = lax.map(one_mode, tangents)
    mixing = jnp.eye(MODES, dtype=jnp.float32) + jnp.triu(coefficients)
    flattened = final.reshape(MODES, -1)
    mixed = jnp.dot(mixing.T, flattened, precision=lax.Precision.HIGHEST, preferred_element_type=jnp.float32)
    return mixed.reshape(final.shape)
```

```python
import functools

import jax
import jax.numpy as jnp
from jax import lax
from jax.experimental import pallas as pl
from jax.experimental.pallas import tpu as pltpu
from jax.sharding import PartitionSpec as P

mean_depth = 1.0
gravity = 1.0
coriolis = 0.5
time_step = 0.5


def padded(cells, sides, width):
    for axis, dim in sides:
        count = lax.axis_size(axis)
        ends = count - 1
        head = lax.slice_in_dim(cells, 0, width, axis=dim)
        tail = lax.slice_in_dim(cells, cells.shape[dim] - width, cells.shape[dim], axis=dim)
        cells = jnp.concatenate(
            [
                lax.ppermute(tail, axis, [(i, (i + 1) % count) for i in range(ends)]),
                cells,
                lax.ppermute(head, axis, [((i + 1) % count, i) for i in range(ends)]),
            ],
            axis=dim,
        )
    return cells


def deriv_x(values):
    return 0.5 * (jnp.roll(values, -1, -1) - jnp.roll(values, 1, -1))


def deriv_y(values):
    return 0.5 * (values[..., 2:, :] - values[..., :-2, :])


def interior(values):
    return values[..., 1:-1, :]


def tendency(base_flow, current):
    depth_total = mean_depth + base_flow[0]
    flow_u = base_flow[1]
    flow_v = base_flow[2]
    height = current[:, 0]
    zonal = current[:, 1]
    meridional = current[:, 2]
    flux_x = depth_total * zonal + height * flow_u
    flux_y = depth_total * meridional + height * flow_v
    height_rate = -(interior(deriv_x(flux_x)) + deriv_y(flux_y))
    zonal_mid = interior(zonal)
    merid_mid = interior(meridional)
    flow_umid = interior(flow_u)
    flow_vmid = interior(flow_v)
    zonal_rate = (
        -(
            flow_umid * interior(deriv_x(zonal))
            + zonal_mid * interior(deriv_x(flow_u))
            + flow_vmid * deriv_y(zonal)
            + merid_mid * deriv_y(flow_u)
        )
        + coriolis * merid_mid
        - gravity * interior(deriv_x(height))
    )
    merid_rate = (
        -(
            flow_umid * interior(deriv_x(meridional))
            + zonal_mid * interior(deriv_x(flow_v))
            + flow_vmid * deriv_y(meridional)
            + merid_mid * deriv_y(flow_v)
        )
        - coriolis * zonal_mid
        - gravity * deriv_y(height)
    )
    return jnp.stack([height_rate, zonal_rate, merid_rate], 1)


def step_wide(base_wide, state_wide, wet_wide):
    slope_one = tendency(base_wide, state_wide)
    middle = wet_wide[1:-1] * (state_wide[:, :, 1:-1] + time_step * slope_one)
    slope_two = tendency(base_wide[:, 1:-1], middle)
    return wet_wide[2:-2] * (
        state_wide[:, :, 2:-2] + 0.5 * time_step * (slope_one[:, :, 1:-1] + slope_two)
    )


def on_device_general(tangents, checkpoints, owner_order, land_mask, coefficients):
    wet_mask = land_mask.astype(jnp.float32)
    current = wet_mask * tangents
    depth = 2
    flows_wide, wet_stack = (
        padded(checkpoints, (("rows", 2),), depth),
        padded(wet_mask[None, None], (("rows", 2),), depth),
    )
    wet_wide = wet_stack[0, 0]

    def fetch_flow(step_index):
        held_tile = lax.dynamic_index_in_dim(flows_wide, owner_order[step_index], 0, keepdims=False)
        return lax.all_gather(held_tile, "mode", axis=2, tiled=True)

    total_steps = owner_order.shape[0]

    def advance(step_index, current):
        widened = padded(current, (("rows", 2),), 2)
        return step_wide(fetch_flow(step_index), widened, wet_wide)

    final = lax.fori_loop(0, total_steps, advance, current)
    mixing = jnp.eye(coefficients.shape[0], dtype=jnp.float32) + jnp.triu(coefficients)
    cell_block = lax.all_to_all(final, "mode", split_axis=3, concat_axis=0, tiled=True)
    flattened = cell_block.reshape(cell_block.shape[0], -1)
    mixed = jnp.dot(
        mixing.T, flattened, precision=lax.Precision.HIGHEST, preferred_element_type=jnp.float32
    )
    return mixed.reshape(cell_block.shape)


LANES = 128
SUB = 8
COEFS = 7


def tile_shift(values, lane, ahead):
    tiles = values.shape[0]
    if ahead:
        rolled = pltpu.roll(values, LANES - 1, 2)
        beside = jnp.concatenate([rolled[1:], rolled[:1]], axis=0) if tiles > 1 else rolled
        return jnp.where(lane == LANES - 1, beside, rolled)
    rolled = pltpu.roll(values, 1, 2)
    beside = jnp.concatenate([rolled[-1:], rolled[:-1]], axis=0) if tiles > 1 else rolled
    return jnp.where(lane == 0, beside, rolled)


def diff_x(values, lane):
    return tile_shift(values, lane, True) - tile_shift(values, lane, False)


def zero_pads(ref, strips):
    lead = ref.shape[:-2]
    edge = jnp.zeros(lead + (SUB, LANES), jnp.float32)
    ref[..., pl.ds(0, SUB), :] = edge
    ref[..., pl.ds(SUB * (strips + 1), SUB), :] = edge


def band(strip, shift=0):
    return pl.ds(SUB * (strip + 1) + shift, SUB)


def build_coefs(order, base_ref, coef, flow_pad, strips, steps, lane):
    zero_pads(flow_pad, strips)

    def one(step, carry):
        slot = order[step]
        for strip in range(strips):
            cells = base_ref[:, strip, slot]
            coef[step, 0, :, pl.ds(SUB * strip, SUB), :] = 0.0625 * (mean_depth + cells[:, 0])
            flow_pad[0, :, band(strip), :] = 0.25 * cells[:, 1]
            flow_pad[1, :, band(strip), :] = 0.25 * cells[:, 2]
        for strip in range(strips):
            rows = pl.ds(SUB * strip, SUB)
            flow_u = flow_pad[0, :, band(strip), :]
            flow_v = flow_pad[1, :, band(strip), :]
            coef[step, 1, :, rows, :] = flow_u
            coef[step, 2, :, rows, :] = flow_v
            coef[step, 3, :, rows, :] = diff_x(flow_u, lane)
            coef[step, 4, :, rows, :] = 0.25 - (
                flow_pad[0, :, band(strip, 1), :] - flow_pad[0, :, band(strip, -1), :]
            )
            coef[step, 5, :, rows, :] = 0.25 + diff_x(flow_v, lane)
            coef[step, 6, :, rows, :] = (
                flow_pad[1, :, band(strip, 1), :] - flow_pad[1, :, band(strip, -1), :]
            )
        return carry

    lax.fori_loop(0, steps, one, 0)


def store_flux(source, flux, coef, step, strip):
    rows = pl.ds(SUB * strip, SUB)
    flux[:, band(strip), :] = (
        coef[step, 0, :, rows, :] * source[2, :, band(strip), :]
        + coef[step, 2, :, rows, :] * source[0, :, band(strip), :]
    )


def scaled_rates(source, flux, coef, step, strip, lane):
    rows = pl.ds(SUB * strip, SUB)
    here, above, below = band(strip), band(strip, 1), band(strip, -1)
    height, zonal, merid = source[0, :, here, :], source[1, :, here, :], source[2, :, here, :]
    depth, flow_u, flow_v, du_dx, turn_v, turn_u, dv_dy = (
        coef[step, i, :, rows, :] for i in range(COEFS)
    )
    flux_x = depth * zonal + flow_u * height
    rate_h = diff_x(flux_x, lane) + (flux[:, above, :] - flux[:, below, :])
    rate_u = turn_v * merid - (
        flow_u * diff_x(zonal, lane)
        + du_dx * zonal
        + flow_v * (source[1, :, above, :] - source[1, :, below, :])
        + diff_x(height, lane)
    )
    rate_v = (
        flow_u * diff_x(merid, lane)
        + turn_u * zonal
        + flow_v * (source[2, :, above, :] - source[2, :, below, :])
        + dv_dy * merid
        + (source[0, :, above, :] - source[0, :, below, :])
    )
    return (height, zonal, merid), (-rate_h, rate_u, -rate_v)


def run_steps(state, middle, flux, coef, wet, strips, steps, lane):
    def one(step, carry):
        for strip in range(strips):
            store_flux(state, flux, coef, step, strip)
        for strip in range(strips):
            held, rates = scaled_rates(state, flux, coef, step, strip, lane)
            water = wet[:, pl.ds(SUB * strip, SUB), :]
            for f in range(3):
                middle[f, :, band(strip), :] = water * (held[f] + rates[f])
        for strip in range(strips):
            store_flux(middle, flux, coef, step, strip)
        for strip in range(strips):
            held, rates = scaled_rates(middle, flux, coef, step, strip, lane)
            water = wet[:, pl.ds(SUB * strip, SUB), :]
            for f in range(3):
                state[f, :, band(strip), :] = state[f, :, band(strip), :] + water * (
                    held[f] + rates[f]
                )
        return carry

    lax.fori_loop(0, steps, one, 0)


def steps_kernel(strips, steps, tiles, order, tan_ref, base_ref, land_ref, out_ref,
                 coef, wet, state, middle, flux, flow_pad):
    lane = lax.broadcasted_iota(jnp.int32, (tiles, SUB, LANES), 2)

    @pl.when(pl.program_id(0) == 0)
    def _():
        for ref in (state, middle, flux):
            zero_pads(ref, strips)
        for strip in range(strips):
            for t in range(tiles):
                wet[t, pl.ds(SUB * strip, SUB), :] = land_ref[
                    strip, :, pl.ds(LANES * t, LANES)
                ].astype(jnp.float32)
        build_coefs(order, base_ref, coef, flow_pad, strips, steps, lane)

    for f, scale in enumerate((0.25, 1.0, 1.0)):
        for strip in range(strips):
            for t in range(tiles):
                state[f, t, band(strip), :] = (
                    scale * wet[t, pl.ds(SUB * strip, SUB), :]
                ) * tan_ref[strip, 0, f, :, pl.ds(LANES * t, LANES)]
    run_steps(state, middle, flux, coef, wet, strips, steps, lane)
    down = 0.5 ** steps
    for f, scale in enumerate((4.0 * down, down, down)):
        for strip in range(strips):
            out_ref[:, strip, 0, f] = scale * state[f, :, band(strip), :]


def step_modes(order, tangents, base, land):
    strips, modes, fields, rows, columns = tangents.shape
    tiles, _, steps = base.shape[:3]
    tall = SUB * (strips + 2)
    return pl.pallas_call(
        functools.partial(steps_kernel, strips, steps, tiles),
        out_shape=jax.ShapeDtypeStruct((tiles, strips, modes, fields, rows, LANES), jnp.float32),
        grid_spec=pltpu.PrefetchScalarGridSpec(
            num_scalar_prefetch=1,
            grid=(modes,),
            in_specs=[
                pl.BlockSpec((strips, 1, fields, rows, columns), lambda k, o: (0, k, 0, 0, 0)),
                pl.BlockSpec(base.shape, lambda k, o: (0,) * 6, pipeline_mode=pl.Buffered(1)),
                pl.BlockSpec(land.shape, lambda k, o: (0,) * 3, pipeline_mode=pl.Buffered(1)),
            ],
            out_specs=pl.BlockSpec(
                (tiles, strips, 1, fields, rows, LANES), lambda k, o: (0, 0, k, 0, 0, 0)
            ),
            scratch_shapes=[
                pltpu.VMEM((steps, COEFS, tiles, SUB * strips, LANES), jnp.float32),
                pltpu.VMEM((tiles, SUB * strips, LANES), jnp.float32),
                pltpu.VMEM((3, tiles, tall, LANES), jnp.float32),
                pltpu.VMEM((3, tiles, tall, LANES), jnp.float32),
                pltpu.VMEM((tiles, tall, LANES), jnp.float32),
                pltpu.VMEM((2, tiles, tall, LANES), jnp.float32),
            ],
        ),
    )(order, tangents, base, land)


def mix_kernel(coef_ref, cells_ref, out_ref):
    modes = coef_ref.shape[0]
    row = lax.broadcasted_iota(jnp.int32, (modes, modes), 0)
    col = lax.broadcasted_iota(jnp.int32, (modes, modes), 1)
    mixing = jnp.where(row <= col, coef_ref[...], 0.0) + jnp.where(row == col, 1.0, 0.0)
    turned = mixing.T
    per = cells_ref.shape[0] // modes
    for spot in range(per):
        cells = cells_ref[pl.ds(spot, modes, stride=per), :]
        out_ref[pl.ds(spot, modes, stride=per), :] = jnp.dot(
            turned, cells, precision=lax.Precision.HIGHEST, preferred_element_type=jnp.float32
        )


def mix(coefficients, cells):
    return pl.pallas_call(
        mix_kernel,
        out_shape=jax.ShapeDtypeStruct(cells.shape, jnp.float32),
        in_specs=[pl.BlockSpec(memory_space=pltpu.VMEM)] * 2,
        out_specs=pl.BlockSpec(memory_space=pltpu.VMEM),
    )(coefficients, cells)


def on_device_whole(tangents, checkpoints, owner_order, land_mask, coefficients):
    strips = lax.axis_size("rows")
    tiles = lax.axis_size("mode")
    held, fields, rows, columns = tangents.shape
    steps = checkpoints.shape[0]
    base = lax.all_gather(checkpoints, ("mode", "rows"))
    base = base.reshape(tiles, strips, steps, fields, rows, LANES)
    land = lax.all_gather(land_mask, "rows")
    whole = lax.all_to_all(tangents, "rows", split_axis=0, concat_axis=0, tiled=True)
    whole = whole.reshape(strips, held // strips, fields, rows, columns)
    done = step_modes(owner_order, whole, base, land)
    done = done.reshape(tiles * strips, held // strips * fields * rows, LANES)
    placed = lax.all_to_all(done, ("mode", "rows"), split_axis=0, concat_axis=0, tiled=True)
    mixed = mix(coefficients, placed.reshape(-1, LANES))
    return mixed.reshape(coefficients.shape[0], fields, rows, LANES)


def on_device(tangents, checkpoints, owner_order, land_mask, coefficients):
    strips = lax.axis_size("rows")
    held, _, rows, columns = tangents.shape
    fits = (
        held % strips == 0 and rows == SUB and checkpoints.shape[-1] == LANES and strips <= 8
        and coefficients.shape[0] % LANES == 0
    )
    chosen = on_device_whole if fits else on_device_general
    return chosen(tangents, checkpoints, owner_order, land_mask, coefficients)


def solution(mesh):
    placed = (
        P("mode", None, "rows", None),
        P(None, None, "rows", "mode"),
        P(),
        P("rows", None),
        P(),
    )
    return jax.shard_map(
        on_device,
        mesh=mesh,
        in_specs=placed,
        out_specs=P(None, None, "rows", "mode"),
        check_vma=False,
    )
```

```python
import functools

import jax
import jax.numpy as jnp
from jax import lax
from jax.experimental import pallas as pl
from jax.experimental.pallas import tpu as pltpu
from jax.sharding import PartitionSpec as P

mean_depth = 1.0
gravity = 1.0
coriolis = 0.5
time_step = 0.5


def padded(cells, sides, width):
    for axis, dim in sides:
        count = lax.axis_size(axis)
        ends = count - 1
        head = lax.slice_in_dim(cells, 0, width, axis=dim)
        tail = lax.slice_in_dim(cells, cells.shape[dim] - width, cells.shape[dim], axis=dim)
        cells = jnp.concatenate(
            [
                lax.ppermute(tail, axis, [(i, (i + 1) % count) for i in range(ends)]),
                cells,
                lax.ppermute(head, axis, [((i + 1) % count, i) for i in range(ends)]),
            ],
            axis=dim,
        )
    return cells


def deriv_x(values):
    return 0.5 * (jnp.roll(values, -1, -1) - jnp.roll(values, 1, -1))


def deriv_y(values):
    return 0.5 * (values[..., 2:, :] - values[..., :-2, :])


def interior(values):
    return values[..., 1:-1, :]


def tendency(base_flow, current):
    depth_total = mean_depth + base_flow[0]
    flow_u = base_flow[1]
    flow_v = base_flow[2]
    height = current[:, 0]
    zonal = current[:, 1]
    meridional = current[:, 2]
    flux_x = depth_total * zonal + height * flow_u
    flux_y = depth_total * meridional + height * flow_v
    height_rate = -(interior(deriv_x(flux_x)) + deriv_y(flux_y))
    zonal_mid = interior(zonal)
    merid_mid = interior(meridional)
    flow_umid = interior(flow_u)
    flow_vmid = interior(flow_v)
    zonal_rate = (
        -(
            flow_umid * interior(deriv_x(zonal))
            + zonal_mid * interior(deriv_x(flow_u))
            + flow_vmid * deriv_y(zonal)
            + merid_mid * deriv_y(flow_u)
        )
        + coriolis * merid_mid
        - gravity * interior(deriv_x(height))
    )
    merid_rate = (
        -(
            flow_umid * interior(deriv_x(meridional))
            + zonal_mid * interior(deriv_x(flow_v))
            + flow_vmid * deriv_y(meridional)
            + merid_mid * deriv_y(flow_v)
        )
        - coriolis * zonal_mid
        - gravity * deriv_y(height)
    )
    return jnp.stack([height_rate, zonal_rate, merid_rate], 1)


def step_wide(base_wide, state_wide, wet_wide):
    slope_one = tendency(base_wide, state_wide)
    middle = wet_wide[1:-1] * (state_wide[:, :, 1:-1] + time_step * slope_one)
    slope_two = tendency(base_wide[:, 1:-1], middle)
    return wet_wide[2:-2] * (
        state_wide[:, :, 2:-2] + 0.5 * time_step * (slope_one[:, :, 1:-1] + slope_two)
    )


def on_device_general(tangents, checkpoints, owner_order, land_mask, coefficients):
    wet_mask = land_mask.astype(jnp.float32)
    current = wet_mask * tangents
    depth = 2
    flows_wide, wet_stack = (
        padded(checkpoints, (("rows", 2),), depth),
        padded(wet_mask[None, None], (("rows", 2),), depth),
    )
    wet_wide = wet_stack[0, 0]

    def fetch_flow(step_index):
        held_tile = lax.dynamic_index_in_dim(flows_wide, owner_order[step_index], 0, keepdims=False)
        return lax.all_gather(held_tile, "mode", axis=2, tiled=True)

    total_steps = owner_order.shape[0]

    def advance(step_index, current):
        widened = padded(current, (("rows", 2),), 2)
        return step_wide(fetch_flow(step_index), widened, wet_wide)

    final = lax.fori_loop(0, total_steps, advance, current)
    mixing = jnp.eye(coefficients.shape[0], dtype=jnp.float32) + jnp.triu(coefficients)
    cell_block = lax.all_to_all(final, "mode", split_axis=3, concat_axis=0, tiled=True)
    flattened = cell_block.reshape(cell_block.shape[0], -1)
    mixed = jnp.dot(
        mixing.T, flattened, precision=lax.Precision.HIGHEST, preferred_element_type=jnp.float32
    )
    return mixed.reshape(cell_block.shape)


LANES = 128
SUB = 8
COEFS = 7


def tile_shift(values, lane, ahead):
    tiles = values.shape[0]
    if ahead:
        rolled = pltpu.roll(values, LANES - 1, 2)
        beside = jnp.concatenate([rolled[1:], rolled[:1]], axis=0) if tiles > 1 else rolled
        return jnp.where(lane == LANES - 1, beside, rolled)
    rolled = pltpu.roll(values, 1, 2)
    beside = jnp.concatenate([rolled[-1:], rolled[:-1]], axis=0) if tiles > 1 else rolled
    return jnp.where(lane == 0, beside, rolled)


def diff_x(values, lane):
    return tile_shift(values, lane, True) - tile_shift(values, lane, False)


def zero_pads(ref, strips):
    lead = ref.shape[:-2]
    edge = jnp.zeros(lead + (SUB, LANES), jnp.float32)
    ref[..., pl.ds(0, SUB), :] = edge
    ref[..., pl.ds(SUB * (strips + 1), SUB), :] = edge


def band(strip, shift=0):
    return pl.ds(SUB * (strip + 1) + shift, SUB)


def build_coefs(order, base_ref, coef, flow_pad, strips, steps, lane):
    zero_pads(flow_pad, strips)

    def one(step, carry):
        first = 3 * order[step]
        for strip in range(strips):
            coef[step, 0, :, pl.ds(SUB * strip, SUB), :] = 0.0625 * (
                mean_depth + base_ref[:, strip, first]
            )
            flow_pad[0, :, band(strip), :] = 0.25 * base_ref[:, strip, first + 1]
            flow_pad[1, :, band(strip), :] = 0.25 * base_ref[:, strip, first + 2]
        for strip in range(strips):
            rows = pl.ds(SUB * strip, SUB)
            flow_u = flow_pad[0, :, band(strip), :]
            flow_v = flow_pad[1, :, band(strip), :]
            coef[step, 1, :, rows, :] = flow_u
            coef[step, 2, :, rows, :] = flow_v
            coef[step, 3, :, rows, :] = diff_x(flow_u, lane)
            coef[step, 4, :, rows, :] = 0.25 - (
                flow_pad[0, :, band(strip, 1), :] - flow_pad[0, :, band(strip, -1), :]
            )
            coef[step, 5, :, rows, :] = 0.25 + diff_x(flow_v, lane)
            coef[step, 6, :, rows, :] = (
                flow_pad[1, :, band(strip, 1), :] - flow_pad[1, :, band(strip, -1), :]
            )
        return carry

    lax.fori_loop(0, steps, one, 0)


def store_flux(source, flux, coef, step, strip):
    rows = pl.ds(SUB * strip, SUB)
    flux[:, band(strip), :] = (
        coef[step, 0, :, rows, :] * source[2, :, band(strip), :]
        + coef[step, 2, :, rows, :] * source[0, :, band(strip), :]
    )


def scaled_rates(source, flux, coef, step, strip, lane):
    rows = pl.ds(SUB * strip, SUB)
    here, above, below = band(strip), band(strip, 1), band(strip, -1)
    height, zonal, merid = source[0, :, here, :], source[1, :, here, :], source[2, :, here, :]
    depth, flow_u, flow_v, du_dx, turn_v, turn_u, dv_dy = (
        coef[step, i, :, rows, :] for i in range(COEFS)
    )
    flux_x = depth * zonal + flow_u * height
    rate_h = diff_x(flux_x, lane) + (flux[:, above, :] - flux[:, below, :])
    rate_u = turn_v * merid - (
        flow_u * diff_x(zonal, lane)
        + du_dx * zonal
        + flow_v * (source[1, :, above, :] - source[1, :, below, :])
        + diff_x(height, lane)
    )
    rate_v = (
        flow_u * diff_x(merid, lane)
        + turn_u * zonal
        + flow_v * (source[2, :, above, :] - source[2, :, below, :])
        + dv_dy * merid
        + (source[0, :, above, :] - source[0, :, below, :])
    )
    return (height, zonal, merid), (-rate_h, rate_u, -rate_v)


def run_steps(state, middle, flux, coef, wet, strips, steps, lane):
    def one(step, carry):
        for strip in range(strips):
            store_flux(state, flux, coef, step, strip)
        for strip in range(strips):
            held, rates = scaled_rates(state, flux, coef, step, strip, lane)
            water = wet[:, pl.ds(SUB * strip, SUB), :]
            for f in range(3):
                middle[f, :, band(strip), :] = water * (held[f] + rates[f])
        for strip in range(strips):
            store_flux(middle, flux, coef, step, strip)
        for strip in range(strips):
            held, rates = scaled_rates(middle, flux, coef, step, strip, lane)
            water = wet[:, pl.ds(SUB * strip, SUB), :]
            for f in range(3):
                state[f, :, band(strip), :] = state[f, :, band(strip), :] + water * (
                    held[f] + rates[f]
                )
        return carry

    lax.fori_loop(0, steps, one, 0)


def steps_kernel(strips, tiles, steps, kept, order, base_ref, land_ref, tan_ref, out_ref,
                 base_all, whole, leaving, coef, wet, state, middle, flux, flow_pad,
                 z_send, z_recv, x_send, x_recv, p_send, p_recv,
                 in_send, in_recv, out_send, out_recv):
    m = lax.axis_index("mode")
    r = lax.axis_index("rows")
    everyone = tiles * strips
    me = m * strips + r
    chips = tiles // 2
    pairs = 2 * (m // 2)
    core = m - pairs
    partner = pairs + 1 - core
    mask_at = 3 * steps
    lane = lax.broadcasted_iota(jnp.int32, (tiles, SUB, LANES), 2)

    def other_chip(j):
        return lax.rem(m + 2 * j, tiles)

    def send(source, target, sent, received, mode, row):
        pltpu.make_async_remote_copy(
            src_ref=source, dst_ref=target, send_sem=sent, recv_sem=received,
            device_id=(mode, row), device_id_type=pl.DeviceIdType.MESH,
        ).start()

    def drain(ref, sem):
        pltpu.make_async_copy(ref, ref, sem).wait()

    barrier = pltpu.get_barrier_semaphore()

    def greet(j, carry):
        target = lax.rem(me + j, everyone)
        pl.semaphore_signal(
            barrier, inc=1, device_id=(target // strips, lax.rem(target, strips)),
            device_id_type=pl.DeviceIdType.MESH,
        )
        return carry

    lax.fori_loop(1, everyone, greet, 0)

    own = base_all.at[m, r]
    own[pl.ds(0, mask_at)] = base_ref[...].reshape(mask_at, SUB, LANES)
    own[mask_at] = land_ref[:, pl.ds(pl.multiple_of(m * LANES, LANES), LANES)].astype(jnp.float32)

    pl.semaphore_wait(barrier, everyone - 1)

    for j in range(1, strips):
        q = lax.rem(r + j, strips)
        send(own, own, z_send, z_recv.at[r], m, q)
    for j in range(1, chips):
        send(own, own, x_send, x_recv.at[m], other_chip(j), r)

    for k in range(kept):
        for j in range(1, strips):
            q = lax.rem(r + j, strips)
            send(tan_ref.at[q * kept + k], whole.at[k, r], in_send, in_recv.at[k], m, q)
        pltpu.make_async_copy(tan_ref.at[r * kept + k], whole.at[k, r], in_recv.at[k]).start()

    for j in range(1, strips):
        q = lax.rem(r + j, strips)
        strip = base_all.at[m, q]
        drain(strip, z_recv.at[q])
        for i in range(1, chips):
            send(strip, strip, x_send, x_recv.at[m], other_chip(i), r)
    send(base_all.at[m], base_all.at[m], p_send, p_recv, partner, r)
    for ref in (state, middle, flux):
        zero_pads(ref, strips)
    for j in range(1, chips):
        tile = other_chip(j)
        drain(base_all.at[tile], x_recv.at[tile])
        send(base_all.at[tile], base_all.at[tile], p_send, p_recv, partner, r)
    drain(base_all.at[pl.ds(0, chips)], p_recv)

    for strip in range(strips):
        wet[:, pl.ds(SUB * strip, SUB), :] = base_all[:, strip, mask_at]
    build_coefs(order, base_all, coef, flow_pad, strips, steps, lane)

    def one_mode(k, carry):
        drain(whole.at[k], in_recv.at[k])
        for f, scale in enumerate((0.25, 1.0, 1.0)):
            for strip in range(strips):
                for t in range(tiles):
                    state[f, t, band(strip), :] = (
                        scale * wet[t, pl.ds(SUB * strip, SUB), :]
                    ) * whole[k, strip, f, :, pl.ds(LANES * t, LANES)]
        run_steps(state, middle, flux, coef, wet, strips, steps, lane)
        down = 0.5 ** steps
        for f, scale in enumerate((4.0 * down, down, down)):
            for strip in range(strips):
                for t in range(tiles):
                    leaving[k, t * strips + strip, f] = scale * state[f, t, band(strip), :]

        def post(j, carry):
            target = lax.rem(me + j, everyone)
            send(leaving.at[k, target], out_ref.at[me, k], out_send, out_recv,
                 target // strips, lax.rem(target, strips))
            return carry

        lax.fori_loop(1, everyone, post, 0)
        pltpu.make_async_copy(leaving.at[k, me], out_ref.at[me, k], out_recv).start()
        return carry

    lax.fori_loop(0, kept, one_mode, 0)

    drain(base_all.at[m, pl.ds(0, strips - 1)], z_send)
    drain(base_all.at[pl.ds(0, chips - 1)], x_send)
    drain(base_all.at[pl.ds(0, chips)], p_send)
    drain(whole.at[:, pl.ds(0, strips - 1)], in_send)
    drain(leaving.at[:, pl.ds(0, everyone - 1)], out_send)
    drain(out_ref, out_recv)


def step_modes(order, base, land, tangents):
    strips, tiles = lax.axis_size("rows"), lax.axis_size("mode")
    held, fields, rows, columns = tangents.shape
    steps = base.shape[0]
    kept = held // strips
    everyone = tiles * strips
    tall = SUB * (strips + 2)
    vmem = pl.BlockSpec(memory_space=pltpu.VMEM)
    anywhere = pl.BlockSpec(memory_space=pl.ANY)
    dma = pltpu.SemaphoreType.DMA
    return pl.pallas_call(
        functools.partial(steps_kernel, strips, tiles, steps, kept),
        out_shape=jax.ShapeDtypeStruct((everyone, kept, fields, rows, LANES), jnp.float32),
        in_specs=[pl.BlockSpec(memory_space=pltpu.SMEM), vmem, vmem, anywhere],
        out_specs=anywhere,
        scratch_shapes=[
            pltpu.VMEM((tiles, strips, steps * fields + 1, rows, LANES), jnp.float32),
            pltpu.VMEM((kept, strips, fields, rows, columns), jnp.float32),
            pltpu.VMEM((kept, everyone, fields, rows, LANES), jnp.float32),
            pltpu.VMEM((steps, COEFS, tiles, SUB * strips, LANES), jnp.float32),
            pltpu.VMEM((tiles, SUB * strips, LANES), jnp.float32),
            pltpu.VMEM((3, tiles, tall, LANES), jnp.float32),
            pltpu.VMEM((3, tiles, tall, LANES), jnp.float32),
            pltpu.VMEM((tiles, tall, LANES), jnp.float32),
            pltpu.VMEM((2, tiles, tall, LANES), jnp.float32),
            dma, dma((strips,)), dma, dma((tiles,)), dma, dma,
            dma, dma((kept,)), dma, dma,
        ],
        compiler_params=pltpu.CompilerParams(collective_id=0, has_side_effects=True),
    )(order, base, land, tangents)


def mix_kernel(coef_ref, cells_ref, out_ref):
    modes = coef_ref.shape[0]
    row = lax.broadcasted_iota(jnp.int32, (modes, modes), 0)
    col = lax.broadcasted_iota(jnp.int32, (modes, modes), 1)
    mixing = jnp.where(row <= col, coef_ref[...], 0.0) + jnp.where(row == col, 1.0, 0.0)
    turned = mixing.T
    per = cells_ref.shape[0] // modes
    for spot in range(per):
        cells = cells_ref[pl.ds(spot, modes, stride=per), :]
        out_ref[pl.ds(spot, modes, stride=per), :] = jnp.dot(
            turned, cells, precision=lax.Precision.HIGHEST, preferred_element_type=jnp.float32
        )


def mix(coefficients, cells):
    return pl.pallas_call(
        mix_kernel,
        out_shape=jax.ShapeDtypeStruct(cells.shape, jnp.float32),
        in_specs=[pl.BlockSpec(memory_space=pltpu.VMEM)] * 2,
        out_specs=pl.BlockSpec(memory_space=pltpu.VMEM),
    )(coefficients, cells)


def on_device_whole(tangents, checkpoints, owner_order, land_mask, coefficients):
    fields, rows = tangents.shape[1:3]
    placed = step_modes(owner_order, checkpoints, land_mask, tangents)
    mixed = mix(coefficients, placed.reshape(-1, LANES))
    return mixed.reshape(coefficients.shape[0], fields, rows, LANES)


def on_device(tangents, checkpoints, owner_order, land_mask, coefficients):
    strips = lax.axis_size("rows")
    held, _, rows, columns = tangents.shape
    fits = (
        held % strips == 0 and strips > 1 and lax.axis_size("mode") % 2 == 0
        and lax.axis_size("mode") > 2 and rows == SUB and checkpoints.shape[-1] == LANES and strips <= 8
        and coefficients.shape[0] % LANES == 0
    )
    chosen = on_device_whole if fits else on_device_general
    return chosen(tangents, checkpoints, owner_order, land_mask, coefficients)


def solution(mesh):
    placed = (
        P("mode", None, "rows", None),
        P(None, None, "rows", "mode"),
        P(),
        P("rows", None),
        P(),
    )
    return jax.shard_map(
        on_device,
        mesh=mesh,
        in_specs=placed,
        out_specs=P(None, None, "rows", "mode"),
        check_vma=False,
    )
```

```python
import functools

import jax
import jax.numpy as jnp
from jax import lax
from jax.experimental import pallas as pl
from jax.experimental.pallas import tpu as pltpu
from jax.sharding import PartitionSpec as P

mean_depth = 1.0
gravity = 1.0
coriolis = 0.5
time_step = 0.5


def padded(cells, sides, width):
    for axis, dim in sides:
        count = lax.axis_size(axis)
        ends = count - 1
        head = lax.slice_in_dim(cells, 0, width, axis=dim)
        tail = lax.slice_in_dim(cells, cells.shape[dim] - width, cells.shape[dim], axis=dim)
        cells = jnp.concatenate(
            [
                lax.ppermute(tail, axis, [(i, (i + 1) % count) for i in range(ends)]),
                cells,
                lax.ppermute(head, axis, [((i + 1) % count, i) for i in range(ends)]),
            ],
            axis=dim,
        )
    return cells


def deriv_x(values):
    return 0.5 * (jnp.roll(values, -1, -1) - jnp.roll(values, 1, -1))


def deriv_y(values):
    return 0.5 * (values[..., 2:, :] - values[..., :-2, :])


def interior(values):
    return values[..., 1:-1, :]


def tendency(base_flow, current):
    depth_total = mean_depth + base_flow[0]
    flow_u = base_flow[1]
    flow_v = base_flow[2]
    height = current[:, 0]
    zonal = current[:, 1]
    meridional = current[:, 2]
    flux_x = depth_total * zonal + height * flow_u
    flux_y = depth_total * meridional + height * flow_v
    height_rate = -(interior(deriv_x(flux_x)) + deriv_y(flux_y))
    zonal_mid = interior(zonal)
    merid_mid = interior(meridional)
    flow_umid = interior(flow_u)
    flow_vmid = interior(flow_v)
    zonal_rate = (
        -(
            flow_umid * interior(deriv_x(zonal))
            + zonal_mid * interior(deriv_x(flow_u))
            + flow_vmid * deriv_y(zonal)
            + merid_mid * deriv_y(flow_u)
        )
        + coriolis * merid_mid
        - gravity * interior(deriv_x(height))
    )
    merid_rate = (
        -(
            flow_umid * interior(deriv_x(meridional))
            + zonal_mid * interior(deriv_x(flow_v))
            + flow_vmid * deriv_y(meridional)
            + merid_mid * deriv_y(flow_v)
        )
        - coriolis * zonal_mid
        - gravity * deriv_y(height)
    )
    return jnp.stack([height_rate, zonal_rate, merid_rate], 1)


def step_wide(base_wide, state_wide, wet_wide):
    slope_one = tendency(base_wide, state_wide)
    middle = wet_wide[1:-1] * (state_wide[:, :, 1:-1] + time_step * slope_one)
    slope_two = tendency(base_wide[:, 1:-1], middle)
    return wet_wide[2:-2] * (
        state_wide[:, :, 2:-2] + 0.5 * time_step * (slope_one[:, :, 1:-1] + slope_two)
    )


def on_device_general(tangents, checkpoints, owner_order, land_mask, coefficients):
    wet_mask = land_mask.astype(jnp.float32)
    current = wet_mask * tangents
    depth = 2
    flows_wide, wet_stack = (
        padded(checkpoints, (("rows", 2),), depth),
        padded(wet_mask[None, None], (("rows", 2),), depth),
    )
    wet_wide = wet_stack[0, 0]

    def fetch_flow(step_index):
        held_tile = lax.dynamic_index_in_dim(flows_wide, owner_order[step_index], 0, keepdims=False)
        return lax.all_gather(held_tile, "mode", axis=2, tiled=True)

    total_steps = owner_order.shape[0]

    def advance(step_index, current):
        widened = padded(current, (("rows", 2),), 2)
        return step_wide(fetch_flow(step_index), widened, wet_wide)

    final = lax.fori_loop(0, total_steps, advance, current)
    mixing = jnp.eye(coefficients.shape[0], dtype=jnp.float32) + jnp.triu(coefficients)
    cell_block = lax.all_to_all(final, "mode", split_axis=3, concat_axis=0, tiled=True)
    flattened = cell_block.reshape(cell_block.shape[0], -1)
    mixed = jnp.dot(
        mixing.T, flattened, precision=lax.Precision.HIGHEST, preferred_element_type=jnp.float32
    )
    return mixed.reshape(cell_block.shape)


LANES = 128
SUB = 8
COEFS = 7


def tile_shift(values, lane, ahead):
    tiles = values.shape[0]
    if ahead:
        rolled = pltpu.roll(values, LANES - 1, 2)
        beside = jnp.concatenate([rolled[1:], rolled[:1]], axis=0) if tiles > 1 else rolled
        return jnp.where(lane == LANES - 1, beside, rolled)
    rolled = pltpu.roll(values, 1, 2)
    beside = jnp.concatenate([rolled[-1:], rolled[:-1]], axis=0) if tiles > 1 else rolled
    return jnp.where(lane == 0, beside, rolled)


def diff_x(values, lane):
    return tile_shift(values, lane, True) - tile_shift(values, lane, False)


def zero_pads(ref, strips):
    lead = ref.shape[:-2]
    edge = jnp.zeros(lead + (SUB, LANES), jnp.float32)
    ref[..., pl.ds(0, SUB), :] = edge
    ref[..., pl.ds(SUB * (strips + 1), SUB), :] = edge


def band(strip, shift=0):
    return pl.ds(SUB * (strip + 1) + shift, SUB)


def build_coefs(order, base_ref, coef, flow_pad, strips, steps, lane):
    zero_pads(flow_pad, strips)

    def one(step, carry):
        first = 3 * order[step]
        for strip in range(strips):
            coef[step, 0, :, pl.ds(SUB * strip, SUB), :] = 0.0625 * (
                mean_depth + base_ref[:, strip, first]
            )
            flow_pad[0, :, band(strip), :] = 0.25 * base_ref[:, strip, first + 1]
            flow_pad[1, :, band(strip), :] = 0.25 * base_ref[:, strip, first + 2]
        for strip in range(strips):
            rows = pl.ds(SUB * strip, SUB)
            flow_u = flow_pad[0, :, band(strip), :]
            flow_v = flow_pad[1, :, band(strip), :]
            coef[step, 1, :, rows, :] = flow_u
            coef[step, 2, :, rows, :] = flow_v
            coef[step, 3, :, rows, :] = diff_x(flow_u, lane)
            coef[step, 4, :, rows, :] = 0.25 - (
                flow_pad[0, :, band(strip, 1), :] - flow_pad[0, :, band(strip, -1), :]
            )
            coef[step, 5, :, rows, :] = 0.25 + diff_x(flow_v, lane)
            coef[step, 6, :, rows, :] = (
                flow_pad[1, :, band(strip, 1), :] - flow_pad[1, :, band(strip, -1), :]
            )
        return carry

    lax.fori_loop(0, steps, one, 0)


def store_flux(source, flux, coef, step, strip):
    rows = pl.ds(SUB * strip, SUB)
    flux[:, band(strip), :] = (
        coef[step, 0, :, rows, :] * source[2, :, band(strip), :]
        + coef[step, 2, :, rows, :] * source[0, :, band(strip), :]
    )


def scaled_rates(source, flux, coef, step, strip, lane):
    rows = pl.ds(SUB * strip, SUB)
    here, above, below = band(strip), band(strip, 1), band(strip, -1)
    height, zonal, merid = source[0, :, here, :], source[1, :, here, :], source[2, :, here, :]
    depth, flow_u, flow_v, du_dx, turn_v, turn_u, dv_dy = (
        coef[step, i, :, rows, :] for i in range(COEFS)
    )
    flux_x = depth * zonal + flow_u * height
    rate_h = diff_x(flux_x, lane) + (flux[:, above, :] - flux[:, below, :])
    rate_u = turn_v * merid - (
        flow_u * diff_x(zonal, lane)
        + du_dx * zonal
        + flow_v * (source[1, :, above, :] - source[1, :, below, :])
        + diff_x(height, lane)
    )
    rate_v = (
        flow_u * diff_x(merid, lane)
        + turn_u * zonal
        + flow_v * (source[2, :, above, :] - source[2, :, below, :])
        + dv_dy * merid
        + (source[0, :, above, :] - source[0, :, below, :])
    )
    return (height, zonal, merid), (-rate_h, rate_u, -rate_v)


def run_steps(state, middle, flux, coef, wet, strips, steps, lane):
    def one(step, carry):
        for strip in range(strips):
            store_flux(state, flux, coef, step, strip)
        for strip in range(strips):
            held, rates = scaled_rates(state, flux, coef, step, strip, lane)
            water = wet[:, pl.ds(SUB * strip, SUB), :]
            for f in range(3):
                middle[f, :, band(strip), :] = water * (held[f] + rates[f])
        for strip in range(strips):
            store_flux(middle, flux, coef, step, strip)
        for strip in range(strips):
            held, rates = scaled_rates(middle, flux, coef, step, strip, lane)
            water = wet[:, pl.ds(SUB * strip, SUB), :]
            for f in range(3):
                state[f, :, band(strip), :] = state[f, :, band(strip), :] + water * (
                    held[f] + rates[f]
                )
        return carry

    lax.fori_loop(0, steps, one, 0)


def steps_kernel(strips, tiles, steps, kept, order, base_ref, land_ref, tan_ref, out_ref,
                 base_all, whole, leaving, coef, wet, state, middle, flux, flow_pad,
                 z_send, z_recv, x_send, x_recv, p_send, p_recv,
                 in_send, in_recv, out_send, out_recv, known):
    m = lax.axis_index("mode")
    r = lax.axis_index("rows")
    everyone = tiles * strips
    me = m * strips + r
    chips = tiles // 2
    pairs = 2 * (m // 2)
    core = m - pairs
    partner = pairs + 1 - core
    mask_at = 3 * steps
    lane = lax.broadcasted_iota(jnp.int32, (tiles, SUB, LANES), 2)

    def other_chip(j):
        return lax.rem(m + 2 * j, tiles)

    def send(source, target, sent, received, mode, row):
        pltpu.make_async_remote_copy(
            src_ref=source, dst_ref=target, send_sem=sent, recv_sem=received,
            device_id=(mode, row), device_id_type=pl.DeviceIdType.MESH,
        ).start()

    def drain(ref, sem):
        pltpu.make_async_copy(ref, ref, sem).wait()

    barrier = pltpu.get_barrier_semaphore()

    def signal(sem, mode, row):
        pl.semaphore_signal(
            sem, inc=1, device_id=(mode, row), device_id_type=pl.DeviceIdType.MESH
        )

    for j in range(1, strips):
        signal(barrier, m, lax.rem(r + j, strips))
    for j in range(1, tiles):
        signal(barrier, lax.rem(m + j, tiles), r)

    own = base_all.at[m, r]
    own[pl.ds(0, mask_at)] = base_ref[...].reshape(mask_at, SUB, LANES)
    own[mask_at] = land_ref[:, pl.ds(pl.multiple_of(m * LANES, LANES), LANES)].astype(jnp.float32)

    pl.semaphore_wait(barrier, strips + tiles - 2)

    def send_in(k, j):
        q = lax.rem(r + j, strips)
        send(tan_ref.at[q * kept + k], whole.at[k, r], in_send, in_recv.at[k], m, q)

    def relay(q):
        strip = base_all.at[m, q]

        @pl.when(jnp.logical_and(q <= r, r < strips - 1))
        def _():
            send(strip, strip, z_send.at[0, q], z_recv.at[q], m, r + 1)

        @pl.when(jnp.logical_and(q >= r, r > 0))
        def _():
            send(strip, strip, z_send.at[1, q], z_recv.at[q], m, r - 1)

        for j in range(1, chips):
            send(strip, strip, x_send, x_recv.at[m], other_chip(j), r)

    relay(r)
    for j in range(1, strips):
        send_in(0, j)

        @pl.when(r >= j)
        def _():
            drain(base_all.at[m, r - j], z_recv.at[r - j])
            relay(r - j)

        @pl.when(r + j < strips)
        def _():
            drain(base_all.at[m, r + j], z_recv.at[r + j])
            relay(r + j)

    for k in range(kept):
        if k > 0:
            for j in range(1, strips):
                send_in(k, j)
        pltpu.make_async_copy(tan_ref.at[r * kept + k], whole.at[k, r], in_recv.at[k]).start()
    for j in range(1, tiles):
        signal(known, lax.rem(m + j, tiles), r)
    send(base_all.at[m], base_all.at[m], p_send, p_recv, partner, r)
    for ref in (state, middle, flux):
        zero_pads(ref, strips)
    for j in range(1, chips):
        tile = other_chip(j)
        drain(base_all.at[tile], x_recv.at[tile])
        send(base_all.at[tile], base_all.at[tile], p_send, p_recv, partner, r)
    drain(base_all.at[pl.ds(0, chips)], p_recv)

    for strip in range(strips):
        wet[:, pl.ds(SUB * strip, SUB), :] = base_all[:, strip, mask_at]
    build_coefs(order, base_all, coef, flow_pad, strips, steps, lane)

    def one_mode(k, carry):
        drain(whole.at[k], in_recv.at[k])
        for f, scale in enumerate((0.25, 1.0, 1.0)):
            for strip in range(strips):
                for t in range(tiles):
                    state[f, t, band(strip), :] = (
                        scale * wet[t, pl.ds(SUB * strip, SUB), :]
                    ) * whole[k, strip, f, :, pl.ds(LANES * t, LANES)]
        run_steps(state, middle, flux, coef, wet, strips, steps, lane)
        down = 0.5 ** steps
        for f, scale in enumerate((4.0 * down, down, down)):
            for strip in range(strips):
                for t in range(tiles):
                    leaving[k, t * strips + strip, f] = scale * state[f, t, band(strip), :]

        def post(j, carry):
            target = lax.rem(me + j, everyone)
            send(leaving.at[k, target], out_ref.at[me, k], out_send, out_recv,
                 target // strips, lax.rem(target, strips))
            return carry

        lax.fori_loop(1, everyone, post, 0)
        pltpu.make_async_copy(leaving.at[k, me], out_ref.at[me, k], out_recv).start()
        return carry

    pl.semaphore_wait(known, tiles - 1)
    lax.fori_loop(0, kept, one_mode, 0)

    for q in range(strips):

        @pl.when(jnp.logical_and(q <= r, r < strips - 1))
        def _():
            drain(base_all.at[m, q], z_send.at[0, q])

        @pl.when(jnp.logical_and(q >= r, r > 0))
        def _():
            drain(base_all.at[m, q], z_send.at[1, q])

    drain(base_all.at[pl.ds(0, chips - 1)], x_send)
    drain(base_all.at[pl.ds(0, chips)], p_send)
    drain(whole.at[:, pl.ds(0, strips - 1)], in_send)
    drain(leaving.at[:, pl.ds(0, everyone - 1)], out_send)
    drain(out_ref, out_recv)


def step_modes(order, base, land, tangents):
    strips, tiles = lax.axis_size("rows"), lax.axis_size("mode")
    held, fields, rows, columns = tangents.shape
    steps = base.shape[0]
    kept = held // strips
    everyone = tiles * strips
    tall = SUB * (strips + 2)
    vmem = pl.BlockSpec(memory_space=pltpu.VMEM)
    anywhere = pl.BlockSpec(memory_space=pl.ANY)
    dma = pltpu.SemaphoreType.DMA
    return pl.pallas_call(
        functools.partial(steps_kernel, strips, tiles, steps, kept),
        out_shape=jax.ShapeDtypeStruct((everyone, kept, fields, rows, LANES), jnp.float32),
        in_specs=[pl.BlockSpec(memory_space=pltpu.SMEM), vmem, vmem, anywhere],
        out_specs=anywhere,
        scratch_shapes=[
            pltpu.VMEM((tiles, strips, steps * fields + 1, rows, LANES), jnp.float32),
            pltpu.VMEM((kept, strips, fields, rows, columns), jnp.float32),
            pltpu.VMEM((kept, everyone, fields, rows, LANES), jnp.float32),
            pltpu.VMEM((steps, COEFS, tiles, SUB * strips, LANES), jnp.float32),
            pltpu.VMEM((tiles, SUB * strips, LANES), jnp.float32),
            pltpu.VMEM((3, tiles, tall, LANES), jnp.float32),
            pltpu.VMEM((3, tiles, tall, LANES), jnp.float32),
            pltpu.VMEM((tiles, tall, LANES), jnp.float32),
            pltpu.VMEM((2, tiles, tall, LANES), jnp.float32),
            dma((2, strips)), dma((strips,)), dma, dma((tiles,)), dma, dma,
            dma, dma((kept,)), dma, dma, pltpu.SemaphoreType.REGULAR,
        ],
        compiler_params=pltpu.CompilerParams(collective_id=0, has_side_effects=True),
    )(order, base, land, tangents)


def halves(values):
    high = values.astype(jnp.bfloat16)
    return high, (values - high.astype(jnp.float32)).astype(jnp.bfloat16)


def mix_kernel(coef_ref, cells_ref, out_ref, turned):
    modes, rows, _ = cells_ref.shape

    @pl.when(pl.program_id(0) == 0)
    def _():
        row = lax.broadcasted_iota(jnp.int32, (modes, modes), 0)
        col = lax.broadcasted_iota(jnp.int32, (modes, modes), 1)
        mixing = jnp.where(row <= col, coef_ref[...], 0.0) + jnp.where(row == col, 1.0, 0.0)
        high, low = halves(mixing.T)
        turned[...] = jnp.concatenate(
            [jnp.concatenate([high, high], 1), jnp.concatenate([low, low], 1)], 0
        )

    cells = cells_ref.reshape(modes * rows, LANES)
    out = out_ref.reshape(modes * rows, LANES)
    for spot in range(0, rows, 2):
        high, low = halves(
            jnp.concatenate([cells[pl.ds(spot + i, modes, stride=rows), :] for i in (0, 1)], 1)
        )
        mixed = jnp.dot(
            turned[...], jnp.concatenate([high, low], 0), preferred_element_type=jnp.float32
        )
        mixed = mixed[:modes] + mixed[modes:]
        for i in (0, 1):
            out[pl.ds(spot + i, modes, stride=rows), :] = mixed[:, LANES * i:LANES * (i + 1)]


def mix(coefficients, cells):
    modes, spots, _ = cells.shape
    return pl.pallas_call(
        mix_kernel,
        out_shape=jax.ShapeDtypeStruct(cells.shape, jnp.float32),
        grid=(spots // SUB,),
        in_specs=[
            pl.BlockSpec((modes, modes), lambda i: (0, 0), pipeline_mode=pl.Buffered(1)),
            pl.BlockSpec((modes, SUB, LANES), lambda i: (0, i, 0)),
        ],
        out_specs=pl.BlockSpec((modes, SUB, LANES), lambda i: (0, i, 0)),
        scratch_shapes=[pltpu.VMEM((2 * modes, 2 * modes), jnp.bfloat16)],
    )(coefficients, cells)


def on_device_whole(tangents, checkpoints, owner_order, land_mask, coefficients):
    fields, rows = tangents.shape[1:3]
    placed = step_modes(owner_order, checkpoints, land_mask, tangents)
    mixed = mix(coefficients, placed.reshape(coefficients.shape[0], fields * rows, LANES))
    return mixed.reshape(coefficients.shape[0], fields, rows, LANES)


def on_device(tangents, checkpoints, owner_order, land_mask, coefficients):
    strips = lax.axis_size("rows")
    held, _, rows, columns = tangents.shape
    fits = (
        held % strips == 0 and strips > 1 and lax.axis_size("mode") % 2 == 0
        and lax.axis_size("mode") > 2 and rows == SUB and checkpoints.shape[-1] == LANES and strips <= 8
        and coefficients.shape[0] % LANES == 0
    )
    chosen = on_device_whole if fits else on_device_general
    return chosen(tangents, checkpoints, owner_order, land_mask, coefficients)


def solution(mesh):
    placed = (
        P("mode", None, "rows", None),
        P(None, None, "rows", "mode"),
        P(),
        P("rows", None),
        P(),
    )
    return jax.shard_map(
        on_device,
        mesh=mesh,
        in_specs=placed,
        out_specs=P(None, None, "rows", "mode"),
        check_vma=False,
    )
```

```python
import functools

import jax
import jax.numpy as jnp
from jax import lax
from jax.experimental import pallas as pl
from jax.experimental.pallas import tpu as pltpu
from jax.sharding import PartitionSpec as P

mean_depth = 1.0
gravity = 1.0
coriolis = 0.5
time_step = 0.5


def padded(cells, sides, width):
    for axis, dim in sides:
        count = lax.axis_size(axis)
        ends = count - 1
        head = lax.slice_in_dim(cells, 0, width, axis=dim)
        tail = lax.slice_in_dim(cells, cells.shape[dim] - width, cells.shape[dim], axis=dim)
        cells = jnp.concatenate(
            [
                lax.ppermute(tail, axis, [(i, (i + 1) % count) for i in range(ends)]),
                cells,
                lax.ppermute(head, axis, [((i + 1) % count, i) for i in range(ends)]),
            ],
            axis=dim,
        )
    return cells


def deriv_x(values):
    return 0.5 * (jnp.roll(values, -1, -1) - jnp.roll(values, 1, -1))


def deriv_y(values):
    return 0.5 * (values[..., 2:, :] - values[..., :-2, :])


def interior(values):
    return values[..., 1:-1, :]


def tendency(base_flow, current):
    depth_total = mean_depth + base_flow[0]
    flow_u = base_flow[1]
    flow_v = base_flow[2]
    height = current[:, 0]
    zonal = current[:, 1]
    meridional = current[:, 2]
    flux_x = depth_total * zonal + height * flow_u
    flux_y = depth_total * meridional + height * flow_v
    height_rate = -(interior(deriv_x(flux_x)) + deriv_y(flux_y))
    zonal_mid = interior(zonal)
    merid_mid = interior(meridional)
    flow_umid = interior(flow_u)
    flow_vmid = interior(flow_v)
    zonal_rate = (
        -(
            flow_umid * interior(deriv_x(zonal))
            + zonal_mid * interior(deriv_x(flow_u))
            + flow_vmid * deriv_y(zonal)
            + merid_mid * deriv_y(flow_u)
        )
        + coriolis * merid_mid
        - gravity * interior(deriv_x(height))
    )
    merid_rate = (
        -(
            flow_umid * interior(deriv_x(meridional))
            + zonal_mid * interior(deriv_x(flow_v))
            + flow_vmid * deriv_y(meridional)
            + merid_mid * deriv_y(flow_v)
        )
        - coriolis * zonal_mid
        - gravity * deriv_y(height)
    )
    return jnp.stack([height_rate, zonal_rate, merid_rate], 1)


def step_wide(base_wide, state_wide, wet_wide):
    slope_one = tendency(base_wide, state_wide)
    middle = wet_wide[1:-1] * (state_wide[:, :, 1:-1] + time_step * slope_one)
    slope_two = tendency(base_wide[:, 1:-1], middle)
    return wet_wide[2:-2] * (
        state_wide[:, :, 2:-2] + 0.5 * time_step * (slope_one[:, :, 1:-1] + slope_two)
    )


def on_device_general(tangents, checkpoints, owner_order, land_mask, coefficients):
    wet_mask = land_mask.astype(jnp.float32)
    current = wet_mask * tangents
    depth = 2
    flows_wide, wet_stack = (
        padded(checkpoints, (("rows", 2),), depth),
        padded(wet_mask[None, None], (("rows", 2),), depth),
    )
    wet_wide = wet_stack[0, 0]

    def fetch_flow(step_index):
        held_tile = lax.dynamic_index_in_dim(flows_wide, owner_order[step_index], 0, keepdims=False)
        return lax.all_gather(held_tile, "mode", axis=2, tiled=True)

    total_steps = owner_order.shape[0]

    def advance(step_index, current):
        widened = padded(current, (("rows", 2),), 2)
        return step_wide(fetch_flow(step_index), widened, wet_wide)

    final = lax.fori_loop(0, total_steps, advance, current)
    mixing = jnp.eye(coefficients.shape[0], dtype=jnp.float32) + jnp.triu(coefficients)
    cell_block = lax.all_to_all(final, "mode", split_axis=3, concat_axis=0, tiled=True)
    flattened = cell_block.reshape(cell_block.shape[0], -1)
    mixed = jnp.dot(
        mixing.T, flattened, precision=lax.Precision.HIGHEST, preferred_element_type=jnp.float32
    )
    return mixed.reshape(cell_block.shape)


LANES = 128
SUB = 8
COEFS = 7


def tile_shift(values, lane, ahead):
    tiles = values.shape[0]
    if ahead:
        rolled = pltpu.roll(values, LANES - 1, 2)
        beside = jnp.concatenate([rolled[1:], rolled[:1]], axis=0) if tiles > 1 else rolled
        return jnp.where(lane == LANES - 1, beside, rolled)
    rolled = pltpu.roll(values, 1, 2)
    beside = jnp.concatenate([rolled[-1:], rolled[:-1]], axis=0) if tiles > 1 else rolled
    return jnp.where(lane == 0, beside, rolled)


def diff_x(values, lane):
    return tile_shift(values, lane, True) - tile_shift(values, lane, False)


def zero_pads(ref, strips):
    lead = ref.shape[:-2]
    edge = jnp.zeros(lead + (SUB, LANES), jnp.float32)
    ref[..., pl.ds(0, SUB), :] = edge
    ref[..., pl.ds(SUB * (strips + 1), SUB), :] = edge


def band(strip, shift=0):
    return pl.ds(SUB * (strip + 1) + shift, SUB)


def build_coefs(order, base_ref, coef, flow_pad, strips, steps, lane):
    zero_pads(flow_pad, strips)

    def one(step, carry):
        first = 3 * order[step]
        for strip in range(strips):
            coef[step, 0, :, pl.ds(SUB * strip, SUB), :] = 0.0625 * (
                mean_depth + base_ref[:, strip, first]
            )
            flow_pad[0, :, band(strip), :] = 0.25 * base_ref[:, strip, first + 1]
            flow_pad[1, :, band(strip), :] = 0.25 * base_ref[:, strip, first + 2]
        for strip in range(strips):
            rows = pl.ds(SUB * strip, SUB)
            flow_u = flow_pad[0, :, band(strip), :]
            flow_v = flow_pad[1, :, band(strip), :]
            coef[step, 1, :, rows, :] = flow_u
            coef[step, 2, :, rows, :] = flow_v
            coef[step, 3, :, rows, :] = diff_x(flow_u, lane)
            coef[step, 4, :, rows, :] = 0.25 - (
                flow_pad[0, :, band(strip, 1), :] - flow_pad[0, :, band(strip, -1), :]
            )
            coef[step, 5, :, rows, :] = 0.25 + diff_x(flow_v, lane)
            coef[step, 6, :, rows, :] = (
                flow_pad[1, :, band(strip, 1), :] - flow_pad[1, :, band(strip, -1), :]
            )
        return carry

    lax.fori_loop(0, steps, one, 0)


def store_flux(source, flux, coef, step, strip):
    rows = pl.ds(SUB * strip, SUB)
    flux[:, band(strip), :] = (
        coef[step, 0, :, rows, :] * source[2, :, band(strip), :]
        + coef[step, 2, :, rows, :] * source[0, :, band(strip), :]
    )


def scaled_rates(source, flux, coef, step, strip, lane):
    rows = pl.ds(SUB * strip, SUB)
    here, above, below = band(strip), band(strip, 1), band(strip, -1)
    height, zonal, merid = source[0, :, here, :], source[1, :, here, :], source[2, :, here, :]
    depth, flow_u, flow_v, du_dx, turn_v, turn_u, dv_dy = (
        coef[step, i, :, rows, :] for i in range(COEFS)
    )
    flux_x = depth * zonal + flow_u * height
    rate_h = diff_x(flux_x, lane) + (flux[:, above, :] - flux[:, below, :])
    rate_u = turn_v * merid - (
        flow_u * diff_x(zonal, lane)
        + du_dx * zonal
        + flow_v * (source[1, :, above, :] - source[1, :, below, :])
        + diff_x(height, lane)
    )
    rate_v = (
        flow_u * diff_x(merid, lane)
        + turn_u * zonal
        + flow_v * (source[2, :, above, :] - source[2, :, below, :])
        + dv_dy * merid
        + (source[0, :, above, :] - source[0, :, below, :])
    )
    return (height, zonal, merid), (-rate_h, rate_u, -rate_v)


def run_steps(state, middle, flux, coef, wet, strips, steps, lane):
    def one(step, carry):
        for strip in range(strips):
            store_flux(state, flux, coef, step, strip)
        for strip in range(strips):
            held, rates = scaled_rates(state, flux, coef, step, strip, lane)
            water = wet[:, pl.ds(SUB * strip, SUB), :]
            for f in range(3):
                middle[f, :, band(strip), :] = water * (held[f] + rates[f])
        for strip in range(strips):
            store_flux(middle, flux, coef, step, strip)
        for strip in range(strips):
            held, rates = scaled_rates(middle, flux, coef, step, strip, lane)
            water = wet[:, pl.ds(SUB * strip, SUB), :]
            for f in range(3):
                state[f, :, band(strip), :] = state[f, :, band(strip), :] + water * (
                    held[f] + rates[f]
                )
        return carry

    lax.fori_loop(0, steps, one, 0)


def steps_kernel(strips, tiles, steps, kept, order_ref, base_ref, land_ref, tan_ref, out_ref,
                 base_all, whole, leaving, coef, wet, state, middle, flux, flow_pad,
                 z_send, z_recv, x_send, x_recv, p_send, p_recv,
                 in_send, in_recv, out_send, out_recv, known, land, order, fetch):
    m = lax.axis_index("mode")
    r = lax.axis_index("rows")
    everyone = tiles * strips
    me = m * strips + r
    chips = tiles // 2
    pairs = 2 * (m // 2)
    core = m - pairs
    partner = pairs + 1 - core
    mask_at = 3 * steps
    lane = lax.broadcasted_iota(jnp.int32, (tiles, SUB, LANES), 2)

    def other_chip(j):
        return lax.rem(m + 2 * j, tiles)

    def send(source, target, sent, received, mode, row):
        pltpu.make_async_remote_copy(
            src_ref=source, dst_ref=target, send_sem=sent, recv_sem=received,
            device_id=(mode, row), device_id_type=pl.DeviceIdType.MESH,
        ).start()

    def drain(ref, sem):
        pltpu.make_async_copy(ref, ref, sem).wait()

    barrier = pltpu.get_barrier_semaphore()

    def signal(sem, mode, row):
        pl.semaphore_signal(
            sem, inc=1, device_id=(mode, row), device_id_type=pl.DeviceIdType.MESH
        )

    for j in range(1, strips):
        signal(barrier, m, lax.rem(r + j, strips))
    for j in range(1, tiles):
        signal(barrier, lax.rem(m + j, tiles), r)

    own = base_all.at[m, r]
    tile_of_land = land_ref.at[:, pl.ds(pl.multiple_of(m * LANES, LANES), LANES)]
    fetch_base = pltpu.make_async_copy(base_ref, own.at[pl.ds(0, mask_at)], fetch.at[0])
    fetch_land = pltpu.make_async_copy(tile_of_land, land, fetch.at[1])
    fetch_order = pltpu.make_async_copy(order_ref, order, fetch.at[2])
    fetch_base.start()
    fetch_land.start()
    fetch_order.start()
    fetch_land.wait()
    own[mask_at] = land[...].astype(jnp.float32)
    fetch_base.wait()
    fetch_order.wait()

    pl.semaphore_wait(barrier, strips + tiles - 2)

    def send_in(k, j):
        q = lax.rem(r + j, strips)
        send(tan_ref.at[q * kept + k], whole.at[k, r], in_send, in_recv.at[k], m, q)

    def relay(q):
        strip = base_all.at[m, q]

        @pl.when(jnp.logical_and(q <= r, r < strips - 1))
        def _():
            send(strip, strip, z_send.at[0, q], z_recv.at[q], m, r + 1)

        @pl.when(jnp.logical_and(q >= r, r > 0))
        def _():
            send(strip, strip, z_send.at[1, q], z_recv.at[q], m, r - 1)

        for j in range(1, chips):
            send(strip, strip, x_send, x_recv.at[m], other_chip(j), r)

    relay(r)
    for j in range(1, strips):
        send_in(0, j)

        @pl.when(r >= j)
        def _():
            drain(base_all.at[m, r - j], z_recv.at[r - j])
            relay(r - j)

        @pl.when(r + j < strips)
        def _():
            drain(base_all.at[m, r + j], z_recv.at[r + j])
            relay(r + j)

    for k in range(kept):
        if k > 0:
            for j in range(1, strips):
                send_in(k, j)
        pltpu.make_async_copy(tan_ref.at[r * kept + k], whole.at[k, r], in_recv.at[k]).start()
    for j in range(1, tiles):
        signal(known, lax.rem(m + j, tiles), r)
    send(base_all.at[m], base_all.at[m], p_send, p_recv, partner, r)
    for ref in (state, middle, flux):
        zero_pads(ref, strips)
    for j in range(1, chips):
        tile = other_chip(j)
        drain(base_all.at[tile], x_recv.at[tile])
        send(base_all.at[tile], base_all.at[tile], p_send, p_recv, partner, r)
    drain(base_all.at[pl.ds(0, chips)], p_recv)

    for strip in range(strips):
        wet[:, pl.ds(SUB * strip, SUB), :] = base_all[:, strip, mask_at]
    build_coefs(order, base_all, coef, flow_pad, strips, steps, lane)

    def one_mode(k, carry):
        drain(whole.at[k], in_recv.at[k])
        for f, scale in enumerate((0.25, 1.0, 1.0)):
            for strip in range(strips):
                for t in range(tiles):
                    state[f, t, band(strip), :] = (
                        scale * wet[t, pl.ds(SUB * strip, SUB), :]
                    ) * whole[k, strip, f, :, pl.ds(LANES * t, LANES)]
        run_steps(state, middle, flux, coef, wet, strips, steps, lane)
        down = 0.5 ** steps
        for f, scale in enumerate((4.0 * down, down, down)):
            for strip in range(strips):
                for t in range(tiles):
                    leaving[k, t * strips + strip, f] = scale * state[f, t, band(strip), :]

        def post(row):
            def to(j, carry):
                mode = lax.rem(m + j, tiles)
                send(leaving.at[k, mode * strips + row], out_ref.at[me, k], out_send, out_recv,
                     mode, row)
                return carry

            return to

        for j in range(strips):
            row = lax.rem(r + strips // 2 + j, strips)
            lax.fori_loop(1 if j == strips - strips // 2 else 0, tiles, post(row), 0)
        pltpu.make_async_copy(leaving.at[k, me], out_ref.at[me, k], out_recv).start()
        return carry

    pl.semaphore_wait(known, tiles - 1)
    lax.fori_loop(0, kept, one_mode, 0)

    for q in range(strips):

        @pl.when(jnp.logical_and(q <= r, r < strips - 1))
        def _():
            drain(base_all.at[m, q], z_send.at[0, q])

        @pl.when(jnp.logical_and(q >= r, r > 0))
        def _():
            drain(base_all.at[m, q], z_send.at[1, q])

    drain(base_all.at[pl.ds(0, chips - 1)], x_send)
    drain(base_all.at[pl.ds(0, chips)], p_send)
    drain(whole.at[:, pl.ds(0, strips - 1)], in_send)
    drain(leaving.at[:, pl.ds(0, everyone - 1)], out_send)
    drain(out_ref, out_recv)


def step_modes(order, base, land, tangents):
    strips, tiles = lax.axis_size("rows"), lax.axis_size("mode")
    held, fields, rows, columns = tangents.shape
    steps = base.shape[0]
    kept = held // strips
    everyone = tiles * strips
    tall = SUB * (strips + 2)
    hbm = pl.BlockSpec(memory_space=pltpu.HBM)
    operands = (order, base.reshape(steps * fields, rows, LANES), land, tangents)
    dma = pltpu.SemaphoreType.DMA
    return pl.pallas_call(
        functools.partial(steps_kernel, strips, tiles, steps, kept),
        out_shape=jax.ShapeDtypeStruct((everyone, kept, fields, rows, LANES), jnp.float32),
        in_specs=[hbm] * 4,
        out_specs=pl.BlockSpec(memory_space=pl.ANY),
        scratch_shapes=[
            pltpu.VMEM((tiles, strips, steps * fields + 1, rows, LANES), jnp.float32),
            pltpu.VMEM((kept, strips, fields, rows, columns), jnp.float32),
            pltpu.VMEM((kept, everyone, fields, rows, LANES), jnp.float32),
            pltpu.VMEM((steps, COEFS, tiles, SUB * strips, LANES), jnp.float32),
            pltpu.VMEM((tiles, SUB * strips, LANES), jnp.float32),
            pltpu.VMEM((3, tiles, tall, LANES), jnp.float32),
            pltpu.VMEM((3, tiles, tall, LANES), jnp.float32),
            pltpu.VMEM((tiles, tall, LANES), jnp.float32),
            pltpu.VMEM((2, tiles, tall, LANES), jnp.float32),
            dma((2, strips)), dma((strips,)), dma, dma((tiles,)), dma, dma,
            dma, dma((kept,)), dma, dma, pltpu.SemaphoreType.REGULAR,
            pltpu.VMEM((rows, LANES), jnp.int32), pltpu.SMEM((steps,), jnp.int32), dma((3,)),
        ],
        compiler_params=pltpu.CompilerParams(
            collective_id=0, has_side_effects=True, vmem_limit_bytes=24 << 20
        ),
    )(*(pltpu.with_memory_space_constraint(held_in_hbm, pltpu.HBM) for held_in_hbm in operands))


def halves(values):
    high = values.astype(jnp.bfloat16)
    return high, (values - high.astype(jnp.float32)).astype(jnp.bfloat16)


def mix_kernel(coef_ref, cells_ref, out_ref, turned):
    modes, rows, _ = out_ref.shape
    spots = cells_ref.shape[1]
    first = rows * pl.program_id(0)

    @pl.when(pl.program_id(0) == 0)
    def _():
        row = lax.broadcasted_iota(jnp.int32, (modes, modes), 0)
        col = lax.broadcasted_iota(jnp.int32, (modes, modes), 1)
        mixing = jnp.where(row <= col, coef_ref[...], 0.0) + jnp.where(row == col, 1.0, 0.0)
        high, low = halves(mixing.T)
        turned[...] = jnp.concatenate(
            [jnp.concatenate([high, high], 1), jnp.concatenate([low, low], 1)], 0
        )

    cells = cells_ref.reshape(modes * spots, LANES)
    out = out_ref.reshape(modes * rows, LANES)
    for spot in range(0, rows, 2):
        high, low = halves(
            jnp.concatenate([cells[pl.ds(first + spot + i, modes, stride=spots), :] for i in (0, 1)], 1)
        )
        mixed = jnp.dot(
            turned[...], jnp.concatenate([high, low], 0), preferred_element_type=jnp.float32
        )
        mixed = mixed[:modes] + mixed[modes:]
        for i in (0, 1):
            out[pl.ds(spot + i, modes, stride=rows), :] = mixed[:, LANES * i:LANES * (i + 1)]


def mix(coefficients, cells):
    modes, spots, _ = cells.shape
    return pl.pallas_call(
        mix_kernel,
        out_shape=jax.ShapeDtypeStruct(cells.shape, jnp.float32),
        grid=(spots // SUB,),
        in_specs=[
            pl.BlockSpec((modes, modes), lambda i: (0, 0), pipeline_mode=pl.Buffered(1)),
            pl.BlockSpec(memory_space=pltpu.VMEM),
        ],
        out_specs=pl.BlockSpec((modes, SUB, LANES), lambda i: (0, i, 0)),
        scratch_shapes=[pltpu.VMEM((2 * modes, 2 * modes), jnp.bfloat16)],
        compiler_params=pltpu.CompilerParams(vmem_limit_bytes=8 << 20),
    )(coefficients, cells)


def on_device_whole(tangents, checkpoints, owner_order, land_mask, coefficients):
    fields, rows = tangents.shape[1:3]
    placed = step_modes(owner_order, checkpoints, land_mask, tangents)
    mixed = mix(coefficients, placed.reshape(coefficients.shape[0], fields * rows, LANES))
    return mixed.reshape(coefficients.shape[0], fields, rows, LANES)


def on_device(tangents, checkpoints, owner_order, land_mask, coefficients):
    strips = lax.axis_size("rows")
    held, _, rows, columns = tangents.shape
    fits = (
        held % strips == 0 and strips > 1 and lax.axis_size("mode") % 2 == 0
        and lax.axis_size("mode") > 2 and rows == SUB and checkpoints.shape[-1] == LANES and strips <= 8
        and coefficients.shape[0] % LANES == 0
    )
    chosen = on_device_whole if fits else on_device_general
    return chosen(tangents, checkpoints, owner_order, land_mask, coefficients)


def solution(mesh):
    placed = (
        P("mode", None, "rows", None),
        P(None, None, "rows", "mode"),
        P(),
        P("rows", None),
        P(),
    )
    return jax.shard_map(
        on_device,
        mesh=mesh,
        in_specs=placed,
        out_specs=P(None, None, "rows", "mode"),
        check_vma=False,
    )
```

```python
import functools

import jax
import jax.numpy as jnp
from jax import lax
from jax.experimental import pallas as pl
from jax.experimental.pallas import tpu as pltpu
from jax.sharding import PartitionSpec as P

mean_depth = 1.0
gravity = 1.0
coriolis = 0.5
time_step = 0.5


def padded(cells, sides, width):
    for axis, dim in sides:
        count = lax.axis_size(axis)
        ends = count - 1
        head = lax.slice_in_dim(cells, 0, width, axis=dim)
        tail = lax.slice_in_dim(cells, cells.shape[dim] - width, cells.shape[dim], axis=dim)
        cells = jnp.concatenate(
            [
                lax.ppermute(tail, axis, [(i, (i + 1) % count) for i in range(ends)]),
                cells,
                lax.ppermute(head, axis, [((i + 1) % count, i) for i in range(ends)]),
            ],
            axis=dim,
        )
    return cells


def deriv_x(values):
    return 0.5 * (jnp.roll(values, -1, -1) - jnp.roll(values, 1, -1))


def deriv_y(values):
    return 0.5 * (values[..., 2:, :] - values[..., :-2, :])


def interior(values):
    return values[..., 1:-1, :]


def tendency(base_flow, current):
    depth_total = mean_depth + base_flow[0]
    flow_u = base_flow[1]
    flow_v = base_flow[2]
    height = current[:, 0]
    zonal = current[:, 1]
    meridional = current[:, 2]
    flux_x = depth_total * zonal + height * flow_u
    flux_y = depth_total * meridional + height * flow_v
    height_rate = -(interior(deriv_x(flux_x)) + deriv_y(flux_y))
    zonal_mid = interior(zonal)
    merid_mid = interior(meridional)
    flow_umid = interior(flow_u)
    flow_vmid = interior(flow_v)
    zonal_rate = (
        -(
            flow_umid * interior(deriv_x(zonal))
            + zonal_mid * interior(deriv_x(flow_u))
            + flow_vmid * deriv_y(zonal)
            + merid_mid * deriv_y(flow_u)
        )
        + coriolis * merid_mid
        - gravity * interior(deriv_x(height))
    )
    merid_rate = (
        -(
            flow_umid * interior(deriv_x(meridional))
            + zonal_mid * interior(deriv_x(flow_v))
            + flow_vmid * deriv_y(meridional)
            + merid_mid * deriv_y(flow_v)
        )
        - coriolis * zonal_mid
        - gravity * deriv_y(height)
    )
    return jnp.stack([height_rate, zonal_rate, merid_rate], 1)


def step_wide(base_wide, state_wide, wet_wide):
    slope_one = tendency(base_wide, state_wide)
    middle = wet_wide[1:-1] * (state_wide[:, :, 1:-1] + time_step * slope_one)
    slope_two = tendency(base_wide[:, 1:-1], middle)
    return wet_wide[2:-2] * (
        state_wide[:, :, 2:-2] + 0.5 * time_step * (slope_one[:, :, 1:-1] + slope_two)
    )


def on_device_general(tangents, checkpoints, owner_order, land_mask, coefficients):
    wet_mask = land_mask.astype(jnp.float32)
    current = wet_mask * tangents
    depth = 2
    flows_wide, wet_stack = (
        padded(checkpoints, (("rows", 2),), depth),
        padded(wet_mask[None, None], (("rows", 2),), depth),
    )
    wet_wide = wet_stack[0, 0]

    def fetch_flow(step_index):
        held_tile = lax.dynamic_index_in_dim(flows_wide, owner_order[step_index], 0, keepdims=False)
        return lax.all_gather(held_tile, "mode", axis=2, tiled=True)

    total_steps = owner_order.shape[0]

    def advance(step_index, current):
        widened = padded(current, (("rows", 2),), 2)
        return step_wide(fetch_flow(step_index), widened, wet_wide)

    final = lax.fori_loop(0, total_steps, advance, current)
    mixing = jnp.eye(coefficients.shape[0], dtype=jnp.float32) + jnp.triu(coefficients)
    cell_block = lax.all_to_all(final, "mode", split_axis=3, concat_axis=0, tiled=True)
    flattened = cell_block.reshape(cell_block.shape[0], -1)
    mixed = jnp.dot(
        mixing.T, flattened, precision=lax.Precision.HIGHEST, preferred_element_type=jnp.float32
    )
    return mixed.reshape(cell_block.shape)


LANES = 128
SUB = 8
COEFS = 7


def tile_shift(values, lane, ahead):
    tiles = values.shape[0]
    if ahead:
        rolled = pltpu.roll(values, LANES - 1, 2)
        beside = jnp.concatenate([rolled[1:], rolled[:1]], axis=0) if tiles > 1 else rolled
        return jnp.where(lane == LANES - 1, beside, rolled)
    rolled = pltpu.roll(values, 1, 2)
    beside = jnp.concatenate([rolled[-1:], rolled[:-1]], axis=0) if tiles > 1 else rolled
    return jnp.where(lane == 0, beside, rolled)


def diff_x(values, lane):
    return tile_shift(values, lane, True) - tile_shift(values, lane, False)


def zero_pads(ref, strips):
    lead = ref.shape[:-2]
    edge = jnp.zeros(lead + (SUB, LANES), jnp.float32)
    ref[..., pl.ds(0, SUB), :] = edge
    ref[..., pl.ds(SUB * (strips + 1), SUB), :] = edge


def band(strip, shift=0):
    return pl.ds(SUB * (strip + 1) + shift, SUB)


def build_coefs(order, base_ref, coef, flow_pad, strips, steps, lane):
    zero_pads(flow_pad, strips)

    def one(step, carry):
        first = 3 * order[step]
        for strip in range(strips):
            coef[step, 0, :, pl.ds(SUB * strip, SUB), :] = 0.0625 * (
                mean_depth + base_ref[:, strip, first]
            )
            flow_pad[0, :, band(strip), :] = 0.25 * base_ref[:, strip, first + 1]
            flow_pad[1, :, band(strip), :] = 0.25 * base_ref[:, strip, first + 2]
        for strip in range(strips):
            rows = pl.ds(SUB * strip, SUB)
            flow_u = flow_pad[0, :, band(strip), :]
            flow_v = flow_pad[1, :, band(strip), :]
            coef[step, 1, :, rows, :] = flow_u
            coef[step, 2, :, rows, :] = flow_v
            coef[step, 3, :, rows, :] = diff_x(flow_u, lane)
            coef[step, 4, :, rows, :] = 0.25 - (
                flow_pad[0, :, band(strip, 1), :] - flow_pad[0, :, band(strip, -1), :]
            )
            coef[step, 5, :, rows, :] = 0.25 + diff_x(flow_v, lane)
            coef[step, 6, :, rows, :] = (
                flow_pad[1, :, band(strip, 1), :] - flow_pad[1, :, band(strip, -1), :]
            )
        return carry

    lax.fori_loop(0, steps, one, 0)


def store_flux(source, flux, coef, step, strip):
    rows = pl.ds(SUB * strip, SUB)
    flux[:, band(strip), :] = (
        coef[step, 0, :, rows, :] * source[2, :, band(strip), :]
        + coef[step, 2, :, rows, :] * source[0, :, band(strip), :]
    )


def scaled_rates(source, flux, coef, step, strip, lane):
    rows = pl.ds(SUB * strip, SUB)
    here, above, below = band(strip), band(strip, 1), band(strip, -1)
    height, zonal, merid = source[0, :, here, :], source[1, :, here, :], source[2, :, here, :]
    depth, flow_u, flow_v, du_dx, turn_v, turn_u, dv_dy = (
        coef[step, i, :, rows, :] for i in range(COEFS)
    )
    flux_x = depth * zonal + flow_u * height
    rate_h = diff_x(flux_x, lane) + (flux[:, above, :] - flux[:, below, :])
    rate_u = turn_v * merid - (
        flow_u * diff_x(zonal, lane)
        + du_dx * zonal
        + flow_v * (source[1, :, above, :] - source[1, :, below, :])
        + diff_x(height, lane)
    )
    rate_v = (
        flow_u * diff_x(merid, lane)
        + turn_u * zonal
        + flow_v * (source[2, :, above, :] - source[2, :, below, :])
        + dv_dy * merid
        + (source[0, :, above, :] - source[0, :, below, :])
    )
    return (height, zonal, merid), (-rate_h, rate_u, -rate_v)


def run_steps(state, middle, flux, coef, wet, strips, steps, lane):
    def one(step, carry):
        for strip in range(strips):
            store_flux(state, flux, coef, step, strip)
        for strip in range(strips):
            held, rates = scaled_rates(state, flux, coef, step, strip, lane)
            water = wet[:, pl.ds(SUB * strip, SUB), :]
            for f in range(3):
                middle[f, :, band(strip), :] = water * (held[f] + rates[f])
        for strip in range(strips):
            store_flux(middle, flux, coef, step, strip)
        for strip in range(strips):
            held, rates = scaled_rates(middle, flux, coef, step, strip, lane)
            water = wet[:, pl.ds(SUB * strip, SUB), :]
            for f in range(3):
                state[f, :, band(strip), :] = state[f, :, band(strip), :] + water * (
                    held[f] + rates[f]
                )
        return carry

    lax.fori_loop(0, steps, one, 0)


def steps_kernel(strips, tiles, steps, kept, order_ref, base_ref, land_ref, tan_ref, out_ref,
                 base_all, whole, leaving, coef, wet, state, middle, flux, flow_pad,
                 z_send, z_recv, x_send, x_recv, p_send, p_recv,
                 in_send, in_recv, out_send, out_recv, known, land, order, fetch):
    m = lax.axis_index("mode")
    r = lax.axis_index("rows")
    everyone = tiles * strips
    me = m * strips + r
    chips = tiles // 2
    pairs = 2 * (m // 2)
    core = m - pairs
    partner = pairs + 1 - core
    mask_at = 3 * steps
    lane = lax.broadcasted_iota(jnp.int32, (tiles, SUB, LANES), 2)

    def other_chip(j):
        return lax.rem(m + 2 * j, tiles)

    def send(source, target, sent, received, mode, row):
        pltpu.make_async_remote_copy(
            src_ref=source, dst_ref=target, send_sem=sent, recv_sem=received,
            device_id=(mode, row), device_id_type=pl.DeviceIdType.MESH,
        ).start()

    def drain(ref, sem):
        pltpu.make_async_copy(ref, ref, sem).wait()

    barrier = pltpu.get_barrier_semaphore()

    def signal(sem, mode, row):
        pl.semaphore_signal(
            sem, inc=1, device_id=(mode, row), device_id_type=pl.DeviceIdType.MESH
        )

    for j in range(1, strips):
        signal(barrier, m, lax.rem(r + j, strips))
    for j in range(1, tiles):
        signal(barrier, lax.rem(m + j, tiles), r)

    own = base_all.at[m, r]
    tile_of_land = land_ref.at[:, pl.ds(pl.multiple_of(m * LANES, LANES), LANES)]
    fetch_base = pltpu.make_async_copy(base_ref, own.at[pl.ds(0, mask_at)], fetch.at[0])
    fetch_land = pltpu.make_async_copy(tile_of_land, land, fetch.at[1])
    fetch_order = pltpu.make_async_copy(order_ref, order, fetch.at[2])
    fetch_base.start()
    fetch_land.start()
    fetch_order.start()
    fetch_land.wait()
    own[mask_at] = land[...].astype(jnp.float32)
    fetch_base.wait()
    fetch_order.wait()

    pl.semaphore_wait(barrier, strips + tiles - 2)

    def send_in(k, j):
        q = lax.rem(r + j, strips)
        send(tan_ref.at[q * kept + k], whole.at[k, r], in_send, in_recv.at[k], m, q)

    def relay(q):
        strip = base_all.at[m, q]

        @pl.when(jnp.logical_and(q <= r, r < strips - 1))
        def _():
            send(strip, strip, z_send.at[0, q], z_recv.at[q], m, r + 1)

        @pl.when(jnp.logical_and(q >= r, r > 0))
        def _():
            send(strip, strip, z_send.at[1, q], z_recv.at[q], m, r - 1)

        for j in range(1, chips):
            send(strip, strip, x_send, x_recv.at[m], other_chip(j), r)

    relay(r)
    for j in range(1, strips):
        send_in(0, j)

        @pl.when(r >= j)
        def _():
            drain(base_all.at[m, r - j], z_recv.at[r - j])
            relay(r - j)

        @pl.when(r + j < strips)
        def _():
            drain(base_all.at[m, r + j], z_recv.at[r + j])
            relay(r + j)

    for k in range(kept):
        if k > 0:
            for j in range(1, strips):
                send_in(k, j)
        pltpu.make_async_copy(tan_ref.at[r * kept + k], whole.at[k, r], in_recv.at[k]).start()
    for j in range(1, tiles):
        signal(known, lax.rem(m + j, tiles), r)
    send(base_all.at[m], base_all.at[m], p_send, p_recv, partner, r)
    for ref in (state, middle, flux):
        zero_pads(ref, strips)
    for j in range(1, chips):
        tile = other_chip(j)
        drain(base_all.at[tile], x_recv.at[tile])
        send(base_all.at[tile], base_all.at[tile], p_send, p_recv, partner, r)
    drain(base_all.at[pl.ds(0, chips)], p_recv)

    for strip in range(strips):
        wet[:, pl.ds(SUB * strip, SUB), :] = base_all[:, strip, mask_at]
    build_coefs(order, base_all, coef, flow_pad, strips, steps, lane)

    def one_mode(k, carry):
        drain(whole.at[k], in_recv.at[k])
        for f, scale in enumerate((0.25, 1.0, 1.0)):
            for strip in range(strips):
                for t in range(tiles):
                    state[f, t, band(strip), :] = (
                        scale * wet[t, pl.ds(SUB * strip, SUB), :]
                    ) * whole[k, strip, f, :, pl.ds(LANES * t, LANES)]
        run_steps(state, middle, flux, coef, wet, strips, steps, lane)
        down = 0.5 ** steps
        for f, scale in enumerate((4.0 * down, down, down)):
            for strip in range(strips):
                for t in range(tiles):
                    leaving[k, t * strips + strip, f] = scale * state[f, t, band(strip), :]

        def post(row):
            def to(j, carry):
                mode = lax.rem(m + j, tiles)
                send(leaving.at[k, mode * strips + row], out_ref.at[me, k], out_send, out_recv,
                     mode, row)
                return carry

            return to

        for j in range(strips):
            row = lax.rem(r + strips // 2 + j, strips)
            lax.fori_loop(1 if j == strips - strips // 2 else 0, tiles, post(row), 0)
        pltpu.make_async_copy(leaving.at[k, me], out_ref.at[me, k], out_recv).start()
        return carry

    pl.semaphore_wait(known, tiles - 1)
    lax.fori_loop(0, kept, one_mode, 0)

    for q in range(strips):

        @pl.when(jnp.logical_and(q <= r, r < strips - 1))
        def _():
            drain(base_all.at[m, q], z_send.at[0, q])

        @pl.when(jnp.logical_and(q >= r, r > 0))
        def _():
            drain(base_all.at[m, q], z_send.at[1, q])

    drain(base_all.at[pl.ds(0, chips - 1)], x_send)
    drain(base_all.at[pl.ds(0, chips)], p_send)
    drain(whole.at[:, pl.ds(0, strips - 1)], in_send)
    drain(leaving.at[:, pl.ds(0, everyone - 1)], out_send)
    drain(out_ref, out_recv)


def step_modes(order, base, land, tangents):
    strips, tiles = lax.axis_size("rows"), lax.axis_size("mode")
    held, fields, rows, columns = tangents.shape
    steps = base.shape[0]
    kept = held // strips
    everyone = tiles * strips
    tall = SUB * (strips + 2)
    hbm = pl.BlockSpec(memory_space=pltpu.HBM)
    operands = (order, base.reshape(steps * fields, rows, LANES), land, tangents)
    dma = pltpu.SemaphoreType.DMA
    return pl.pallas_call(
        functools.partial(steps_kernel, strips, tiles, steps, kept),
        out_shape=jax.ShapeDtypeStruct((everyone, kept, fields, rows, LANES), jnp.float32),
        in_specs=[hbm] * 4,
        out_specs=pl.BlockSpec(memory_space=pl.ANY),
        scratch_shapes=[
            pltpu.VMEM((tiles, strips, steps * fields + 1, rows, LANES), jnp.float32),
            pltpu.VMEM((kept, strips, fields, rows, columns), jnp.float32),
            pltpu.VMEM((kept, everyone, fields, rows, LANES), jnp.float32),
            pltpu.VMEM((steps, COEFS, tiles, SUB * strips, LANES), jnp.float32),
            pltpu.VMEM((tiles, SUB * strips, LANES), jnp.float32),
            pltpu.VMEM((3, tiles, tall, LANES), jnp.float32),
            pltpu.VMEM((3, tiles, tall, LANES), jnp.float32),
            pltpu.VMEM((tiles, tall, LANES), jnp.float32),
            pltpu.VMEM((2, tiles, tall, LANES), jnp.float32),
            dma((2, strips)), dma((strips,)), dma, dma((tiles,)), dma, dma,
            dma, dma((kept,)), dma, dma, pltpu.SemaphoreType.REGULAR,
            pltpu.VMEM((rows, LANES), jnp.int32), pltpu.SMEM((steps,), jnp.int32), dma((3,)),
        ],
        compiler_params=pltpu.CompilerParams(
            collective_id=0, has_side_effects=True, vmem_limit_bytes=24 << 20
        ),
    )(*(pltpu.with_memory_space_constraint(held_in_hbm, pltpu.HBM) for held_in_hbm in operands))


def halves(values):
    high = values.astype(jnp.bfloat16)
    return high, (values - high.astype(jnp.float32)).astype(jnp.bfloat16)


def mix_kernel(coef_ref, cells_ref, out_ref, staged, sems):
    modes, spots, _ = cells_ref.shape
    row = lax.broadcasted_iota(jnp.int32, (modes, modes), 0)
    col = lax.broadcasted_iota(jnp.int32, (modes, modes), 1)
    mixing = jnp.where(row <= col, coef_ref[...], 0.0) + jnp.where(row == col, 1.0, 0.0)
    high, low = halves(mixing.T)
    turned = jnp.concatenate(
        [jnp.concatenate([high, high], 1), jnp.concatenate([low, low], 1)], 0
    )
    cells = cells_ref.reshape(modes * spots, LANES)
    copies = []
    for group in range(spots // SUB):
        out = staged.at[group].reshape(modes * SUB, LANES)
        for spot in range(0, SUB, 2):
            first = SUB * group + spot
            high, low = halves(jnp.concatenate(
                [cells[pl.ds(first + i, modes, stride=spots), :] for i in (0, 1)], 1
            ))
            mixed = jnp.dot(
                turned, jnp.concatenate([high, low], 0), preferred_element_type=jnp.float32
            )
            mixed = mixed[:modes] + mixed[modes:]
            for i in (0, 1):
                out[pl.ds(spot + i, modes, stride=SUB), :] = mixed[:, LANES * i:LANES * (i + 1)]
        copies.append(pltpu.make_async_copy(
            staged.at[group], out_ref.at[:, pl.ds(SUB * group, SUB)], sems.at[group]
        ))
        copies[-1].start()
    for copy in copies:
        copy.wait()


def mix(coefficients, cells):
    modes, spots, _ = cells.shape
    return pl.pallas_call(
        mix_kernel,
        out_shape=jax.ShapeDtypeStruct(cells.shape, jnp.float32),
        in_specs=[pl.BlockSpec(memory_space=pltpu.VMEM)] * 2,
        out_specs=pl.BlockSpec(memory_space=pltpu.HBM),
        scratch_shapes=[
            pltpu.VMEM((spots // SUB, modes, SUB, LANES), jnp.float32),
            pltpu.SemaphoreType.DMA((spots // SUB,)),
        ],
        compiler_params=pltpu.CompilerParams(vmem_limit_bytes=8 << 20),
    )(coefficients, cells)


def on_device_whole(tangents, checkpoints, owner_order, land_mask, coefficients):
    fields, rows = tangents.shape[1:3]
    placed = step_modes(owner_order, checkpoints, land_mask, tangents)
    mixed = mix(coefficients, placed.reshape(coefficients.shape[0], fields * rows, LANES))
    return mixed.reshape(coefficients.shape[0], fields, rows, LANES)


def on_device(tangents, checkpoints, owner_order, land_mask, coefficients):
    strips = lax.axis_size("rows")
    held, _, rows, columns = tangents.shape
    fits = (
        held % strips == 0 and strips > 1 and lax.axis_size("mode") % 2 == 0
        and lax.axis_size("mode") > 2 and rows == SUB and checkpoints.shape[-1] == LANES and strips <= 8
        and coefficients.shape[0] % LANES == 0
    )
    chosen = on_device_whole if fits else on_device_general
    return chosen(tangents, checkpoints, owner_order, land_mask, coefficients)


def solution(mesh):
    placed = (
        P("mode", None, "rows", None),
        P(None, None, "rows", "mode"),
        P(),
        P("rows", None),
        P(),
    )
    return jax.shard_map(
        on_device,
        mesh=mesh,
        in_specs=placed,
        out_specs=P(None, None, "rows", "mode"),
        check_vma=False,
    )
```
